256 devices in a mesh: dp: 8 (over x, y_hi), mp: 32 (over z, y_lo, core).
Axes of the slice: x: 4, y: 4 (y_hi: 2, y_lo: 2; y = y_hi * 2 + y_lo), z: 8, core: 2. Of those that a mesh axis runs over, the one named last changes fastest.
Arguments:
- hidden: bfloat16 [64, 128, 18432], P('dp', None, 'mp'), may hold values from -400 to 400
- cotangent: bfloat16 [64, 128, 4608], P('dp', 'mp'), may hold values from -8 to 8
- w_down: bfloat16 [18432, 4608], P('mp', 'dp'), may hold values from -0.046875 to 0.046875
- lengths: int32 [64], P('dp'), may hold values from 1 to 128, 6144 in all
Outputs:
- weight_grad: float32 [18432, 4608], P('mp', 'dp')
- d_hidden: bfloat16 [64, 128, 18432], P('dp', None, 'mp')
The draws below stay inside these ranges and needn't reach their ends.
All inputs are finite; a program needn't handle non-finite values. No bound on the sum of `lengths` on one device may be relied on, other than what follows from the above.
Results may differ from the reference program's by a relative error of at most 0.003.
Values may be sent and summed in bfloat16 or wider, within the bound.
No kernel may reach another device: no remote copies, remote signals or barrier semaphores. Data moves between devices by JAX's collectives and lax.ppermute only.
A program may use at most 256 MiB of HBM per device.

```python
import math
import jax
import jax.numpy as jnp
import numpy as np
from jax import lax

D = 4608
FF = 18432
SEQ = 128
BATCH = 64


def draw_hidden(key, part):
    key_base = jax.random.fold_in(key, 11)
    key_rows = jax.random.fold_in(key, 12)
    key_cols = jax.random.fold_in(key, 13)
    key_common = jax.random.fold_in(key, 14)
    rising = jnp.arange(FF, dtype=jnp.float32) / FF
    base = jax.random.truncated_normal(key_base, -4.0, 4.0, (BATCH, SEQ, FF), jnp.float32)
    col_power = 0.5 * rising + 0.5 * jax.random.uniform(key_cols, (FF,), jnp.float32)
    common = 2.0 * jax.random.truncated_normal(key_common, -4.0, 4.0, (BATCH, 1, FF), jnp.float32)
    row_power = jax.random.uniform(key_rows, (BATCH, SEQ, 1), jnp.float32)
    mixed = 0.8 * base * jnp.power(10.0, row_power) + common
    return (mixed * jnp.power(10.0, col_power)[None, None, :]).astype(jnp.bfloat16)


def draw_cotangent(key, part):
    key_base = jax.random.fold_in(key, 21)
    key_common = jax.random.fold_in(key, 22)
    base = jax.random.truncated_normal(key_base, -4.0, 4.0, (BATCH, SEQ, D), jnp.float32)
    common = jax.random.truncated_normal(key_common, -4.0, 4.0, (BATCH, 1, D), jnp.float32)
    return (base + common).astype(jnp.bfloat16)


def block_scale(key, extent, shards, smallest, largest):
    factor_of = 1.0
    for dim, blocks in shards:
        draws = jax.random.uniform(jax.random.fold_in(jax.random.fold_in(key, 6), dim), (blocks,), jnp.float32, smallest / len(shards), largest / len(shards))
        factor_of = factor_of * jnp.repeat(jnp.exp(draws), extent[dim] // blocks).reshape((-1,) + (1,) * (len(extent) - 1 - dim))
    return factor_of


def split_up(count, total, most, skew):
    weights = [(1 << 20) // math.isqrt(rank ** skew) + 1 for rank in range(2, count + 1)]
    spare, holding = total - most - (count - 1), [1] * (count - 1)
    while spare > 0:
        candidates = [i for i in range(count - 1) if holding[i] < most]
        whole, budget = sum([weights[i] for i in candidates]), spare
        for i in candidates:
            extra = min(most - holding[i], max(1, budget * weights[i] // whole), spare)
            holding[i] = holding[i] + extra
            spare = spare - extra
    return np.array([most] + holding)


def uneven_parts(own_key, number_of, total, reach, slope):
    if number_of == 2:
        one = jax.random.randint(own_key, (), max(1, total - reach), min(reach, total - 1) + 1)
        return jnp.stack([one, total - one])
    tallies = jnp.asarray(split_up(number_of, total, reach, slope), jnp.int32)
    twos = (number_of - 1) // 2
    giver, receiver = tallies[1:1 + 2 * twos:2], tallies[2:2 + 2 * twos:2]
    room = jnp.minimum(giver - 1, reach - receiver)
    shifted = jax.random.randint(jax.random.fold_in(own_key, 1), (twos,), 0, 1 << 20) % (room + 1)
    tallies = tallies.at[1:1 + 2 * twos:2].set(giver - shifted).at[2:2 + 2 * twos:2].set(receiver + shifted)
    return tallies[jax.random.permutation(jax.random.fold_in(own_key, 2), number_of)]


def bell_draw(rng, extent, scale, bound, cuts=(), kind=jnp.bfloat16):
    array = scale * jax.random.normal(rng, extent, jnp.float32)
    if cuts:
        array = array * block_scale(rng, extent, cuts, -0.22, 0.18)
    return jnp.clip(array, -bound, bound).astype(kind)


def setup_inputs(seed: int = 0) -> dict:
    arg_keys = jax.random.split(jax.random.key(seed), 5)
    hidden = draw_hidden(jax.random.fold_in(arg_keys[4], 71), 0)
    cotangent = draw_cotangent(jax.random.fold_in(arg_keys[4], 71), 0)
    w_down = bell_draw(arg_keys[2], (FF, D), FF ** -0.5, 0.046875, ((0, 32), (1, 8)))
    lengths = uneven_parts(arg_keys[3], BATCH, BATCH * SEQ * 3 // 4, SEQ, 1).astype(jnp.int32)
    return {"hidden": hidden, "cotangent": cotangent, "w_down": w_down, "lengths": lengths}


def reference(hidden, cotangent, w_down, lengths):
    positions = jnp.arange(SEQ, dtype=jnp.int32)
    keep = positions[None, :] < lengths[:, None]
    masked = jnp.where(keep[:, :, None], cotangent, jnp.zeros((), cotangent.dtype))
    flat = masked.reshape(BATCH * SEQ, D)
    d_hidden = jnp.dot(flat, w_down.T, preferred_element_type=jnp.float32).astype(jnp.bfloat16)
    d_hidden = d_hidden.reshape(BATCH, SEQ, FF)
    hid_f = hidden.astype(jnp.float32)
    cot_f = masked.astype(jnp.float32)
    hid_gram = jnp.einsum('bsf,btf->bst', hid_f, hid_f, precision=lax.Precision.HIGHEST)
    cot_gram = jnp.einsum('bsd,btd->bst', cot_f, cot_f, precision=lax.Precision.HIGHEST)
    sq_norm = lax.optimization_barrier(jnp.sum(hid_gram * cot_gram, axis=(1, 2)))
    radius = math.sqrt(FF * D / BATCH)
    clip_scale = radius / jnp.sqrt(sq_norm + 1e-06)
    weight_grad = jnp.einsum('bsf,bsd->fd', hid_f, cot_f * clip_scale[:, None, None], precision=lax.Precision.HIGHEST)
    return (weight_grad, d_hidden)
```

```python
import math

import jax
import jax.numpy as jnp
from jax import lax
from jax.experimental import pallas as pl
from jax.experimental.pallas import tpu as pltpu
from jax.sharding import Mesh
from jax.sharding import PartitionSpec as P


TOK = 128
BLK = 576
MAIN = 512
TAIL = BLK - MAIN
HALF = 4 * BLK
F32 = jnp.float32
BF16 = jnp.bfloat16


def nt(a, b):
    return lax.dot_general(a, b, (((1,), (1,)), ((), ())), preferred_element_type=F32)


def tn(a, b):
    return lax.dot_general(a, b, (((0,), (0,)), ((), ())), preferred_element_type=F32)


def nn(a, b):
    return lax.dot_general(a, b, (((1,), (0,)), ((), ())), preferred_element_type=F32)


def gram_kernel(g_ref, h_ref, o_ref):
    for i in range(g_ref.shape[1]):
        m = g_ref[:, i].reshape(TOK, HALF)
        cot = nt(m, m)
        hid = tn(h_ref[i], h_ref[i])
        o_ref[i] = (cot * hid).reshape(TOK // 8, 8, TOK).sum(0)


def gram(g, h):
    step = 2
    n = h.shape[0]
    return pl.pallas_call(
        gram_kernel,
        out_shape=jax.ShapeDtypeStruct((n, 8, TOK), F32),
        grid=(n // step,),
        in_specs=[
            pl.BlockSpec((8, step, 16, HALF), lambda b: (0, b, 0, 0)),
            pl.BlockSpec((step, BLK, TOK), lambda b: (b, 0, 0)),
        ],
        out_specs=pl.BlockSpec((step, 8, TOK), lambda b: (b, 0, 0)),
        cost_estimate=pl.CostEstimate(
            flops=2 * n * TOK * TOK * (HALF + BLK), bytes_accessed=n * TOK * (HALF + BLK) * 2, transcendentals=0
        ),
        name="gram",
    )(g, h)


def wgrad_kernel(dest_ref, g_ref, t_ref, h_ref, clip_ref, o_ref, acc, tail):
    step = pl.program_id(0)
    n = h_ref.shape[0]
    a = jnp.concatenate(
        [(h_ref[i].astype(F32) * clip_ref[step * n + i]).astype(BF16) for i in range(n)], axis=1
    )
    b = jnp.concatenate([g_ref[:, i].reshape(TOK, MAIN) for i in range(n)], axis=0)
    t = jnp.concatenate([t_ref[:, i].reshape(TOK, 128) for i in range(n)], axis=0)
    pm = nn(a, b)
    pt = nn(a, t)

    @pl.when(step == 0)
    def _():
        acc[...] = pm
        tail[...] = pt

    @pl.when(step > 0)
    def _():
        acc[...] += pm
        tail[...] += pt

    @pl.when(step == pl.num_programs(0) - 1)
    def _():
        o_ref[:, :MAIN] = acc[...].astype(o_ref.dtype)
        v = tail[...]
        v = jnp.where(dest_ref[0] % 2 == 1, pltpu.roll(v, TAIL, 1), v)
        o_ref[:, MAIN:] = v[:, :TAIL].astype(o_ref.dtype)


def wgrad(dest, g, h, clip, dtype):
    n = h.shape[0]
    step = 4
    return pl.pallas_call(
        wgrad_kernel,
        out_shape=jax.ShapeDtypeStruct((BLK, BLK), dtype),
        grid_spec=pltpu.PrefetchScalarGridSpec(
            num_scalar_prefetch=1,
            grid=(n // step,),
            in_specs=[
                pl.BlockSpec((8, step, 16, MAIN), lambda b, d: (0, b, 0, d[0])),
                pl.BlockSpec((8, step, 16, 128), lambda b, d: (0, b, 0, 4 * MAIN // 128 + d[0] // 2)),
                pl.BlockSpec((step, BLK, TOK), lambda b, d: (b, 0, 0)),
                pl.BlockSpec(memory_space=pltpu.SMEM),
            ],
            out_specs=pl.BlockSpec((BLK, BLK), lambda b, d: (0, 0)),
            scratch_shapes=[pltpu.VMEM((BLK, MAIN), F32), pltpu.VMEM((BLK, 128), F32)],
        ),
        cost_estimate=pl.CostEstimate(
            flops=2 * n * TOK * BLK * 640, bytes_accessed=n * TOK * (640 + BLK) * 2 + BLK * BLK * 4, transcendentals=0
        ),
        name="wgrad",
    )(dest, g, g, h, clip)


def dhid_kernel(s_ref, g_ref, w0, w1, w2, w3, wt_ref, o_ref):
    for i in range(g_ref.shape[1]):
        total = nt(wt_ref[...], g_ref[:, i, :, 4 * MAIN :].reshape(TOK, 4 * TAIL))
        for k, w in enumerate((w0, w1, w2, w3)):
            off = pl.multiple_of(lax.rem(s_ref[1] + 4 - k, 4) * MAIN, MAIN)
            total += nt(w[:, :MAIN], g_ref[:, i, :, pl.ds(off, MAIN)].reshape(TOK, MAIN))
        o_ref[i] = total.astype(o_ref.dtype)


def dhid(group, x, g, ws, wt, dtype):
    step = 2
    n = 8
    full = pl.BlockSpec((BLK, BLK), lambda b, s: (0, 0))
    return pl.pallas_call(
        dhid_kernel,
        out_shape=jax.ShapeDtypeStruct((n, BLK, TOK), dtype),
        grid_spec=pltpu.PrefetchScalarGridSpec(
            num_scalar_prefetch=1,
            grid=(n // step,),
            in_specs=[
                pl.BlockSpec((8, step, 16, HALF), lambda b, s: (0, s[0] * (n // step) + b, 0, 0)),
                full,
                full,
                full,
                full,
                pl.BlockSpec((BLK, 4 * TAIL), lambda b, s: (0, 0)),
            ],
            out_specs=pl.BlockSpec((step, BLK, TOK), lambda b, s: (b, 0, 0)),
        ),
        cost_estimate=pl.CostEstimate(
            flops=2 * n * TOK * BLK * HALF, bytes_accessed=n * TOK * HALF * 2 + BLK * HALF * 2, transcendentals=0
        ),
        name="dhid",
    )(jnp.stack([group, x]).astype(jnp.int32), g, *ws, wt)


def body(hidden, cotangent, w_down, lengths):
    xi, yh, zi, yl, ci = (lax.axis_index(a) for a in ("x", "yh", "z", "yl", "c"))
    seqs, slots, width = cotangent.shape
    units = hidden.shape[2]

    pos = ((zi * 2 + yl) * 2 + ci) * slots + jnp.arange(slots, dtype=jnp.int32)
    keep = pos[None, :] < lengths[:, None]
    masked = jnp.where(keep[:, :, None], cotangent, jnp.zeros((), cotangent.dtype))

    def half(h):
        at = [(2 * x + h) * BLK for x in range(4)]
        return jnp.concatenate(
            [masked[:, :, o : o + MAIN] for o in at] + [masked[:, :, o + MAIN : o + BLK] for o in at], axis=2
        )

    h0, h1 = half(0), half(1)
    to_send = (jnp.where(ci == 0, h0, h1), jnp.where(ci == 0, h1, h0))

    got = {}
    for k1 in range(2):
        for k2 in range(2):
            perm = []
            for a in range(2):
                for b in range(2):
                    for c in range(2):
                        perm.append((a * 4 + b * 2 + c, (c ^ k1) * 4 + (b ^ k2) * 2 + a))
            got[k1, k2] = lax.ppermute(to_send[k1], ("yh", "yl", "c"), perm)
    rows = []
    for q in range(2):
        for p in range(2):
            s0 = jnp.where(yl == 0, got[p, q], got[p, q ^ 1])
            s1 = jnp.where(yl == 0, got[p ^ 1, q], got[p ^ 1, q ^ 1])
            rows.append(jnp.where(yh == 0, s0, s1))
    block = jnp.concatenate(rows, axis=1)
    g = lax.all_gather(block, ("z", "c"), axis=0, tiled=False)
    g = g.reshape(8, 2 * seqs, 16, HALF)

    ht = jnp.swapaxes(hidden, 1, 2)
    other = lax.ppermute(ht, "yh", [(0, 1), (1, 0)])
    hid = jnp.concatenate([jnp.where(yh == 0, ht, other), jnp.where(yh == 0, other, ht)], axis=0)

    ws = [w_down] + [lax.ppermute(w_down, "x", [(i, (i + k) % 4) for i in range(4)]) for k in range(1, 4)]
    tails = [w[:, MAIN:] for w in ws]
    nat = []
    for x in range(4):
        v = tails[x]
        for me in (1, 2, 3):
            v = jnp.where(xi == me, tails[(me - x) % 4], v)
        if x:
            v = jnp.where(xi == 0, tails[(-x) % 4], v)
        nat.append(v)
    wt = jnp.concatenate(nat, axis=1)

    part = jnp.sum(gram(g, hid), axis=(1, 2))
    mine = jnp.broadcast_to(jnp.pad(part, (0, 128 - 2 * seqs))[None], (64, 128))
    every = lax.all_to_all(mine, ("yh", "z", "yl", "c"), 0, 0, tiled=True)
    sq_norm = jnp.sum(every, axis=0)[: 2 * seqs]
    full_units = units * 32
    radius = math.sqrt(full_units * width / (seqs * 8))
    clip = radius / jnp.sqrt(sq_norm + 1e-06)

    got_w = []
    for k in (2, 1, 3):
        dest = lax.rem(xi + k, 4).reshape(1).astype(jnp.int32)
        piece = wgrad(dest, g, hid, clip, BF16)
        got_w.append(lax.ppermute(piece, "x", [(i, (i + k) % 4) for i in range(4)]))
    own = wgrad(xi.reshape(1).astype(jnp.int32), g, hid, clip, F32)
    weight_grad = own
    for v in got_w:
        weight_grad = weight_grad + v.astype(F32)

    theirs = dhid(1 - yh, xi, g, ws, wt, BF16)
    from_other = lax.ppermute(theirs, "yh", [(0, 1), (1, 0)])
    ours = dhid(yh, xi, g, ws, wt, F32)
    d_hidden = (ours + from_other.astype(F32)).astype(BF16)
    return weight_grad, jnp.swapaxes(d_hidden, 1, 2)


def solution(mesh):
    fine = Mesh(mesh.devices.reshape(4, 2, 8, 2, 2), ("x", "yh", "z", "yl", "c"))
    dp, mp = ("x", "yh"), ("z", "yl", "c")
    in_specs = (P(dp, None, mp), P(dp, mp, None), P(mp, dp), P(dp))
    out_specs = (P(mp, dp), P(dp, None, mp))
    return jax.shard_map(body, mesh=fine, in_specs=in_specs, out_specs=out_specs, check_vma=False)
```

```python
import math

import jax
import jax.numpy as jnp
from jax import lax
from jax.experimental import pallas as pl
from jax.experimental.pallas import tpu as pltpu
from jax.sharding import Mesh
from jax.sharding import PartitionSpec as P


TOK = 128
BLK = 576
MAIN = 512
TAIL = BLK - MAIN
HALF = 4 * BLK
ROWS = 16
F32 = jnp.float32
BF16 = jnp.bfloat16


def nt(a, b):
    return lax.dot_general(a, b, (((1,), (1,)), ((), ())), preferred_element_type=F32)


def tn(a, b):
    return lax.dot_general(a, b, (((0,), (0,)), ((), ())), preferred_element_type=F32)


def nn(a, b):
    return lax.dot_general(a, b, (((1,), (0,)), ((), ())), preferred_element_type=F32)


def cost(flops, moved):
    return pl.CostEstimate(flops=int(flops), bytes_accessed=int(moved), transcendentals=0)


VM = pl.BlockSpec(memory_space=pltpu.VMEM)
ANY = pl.BlockSpec(memory_space=pl.ANY)
HBM = pl.BlockSpec(memory_space=pltpu.HBM)
SM = pl.BlockSpec(memory_space=pltpu.SMEM)


def limit(mib):
    return pltpu.CompilerParams(vmem_limit_bytes=mib * 2**20)


def hgram_kernel(h_ref, o_ref):
    @pl.loop(0, h_ref.shape[0] // 2)
    def _(b):
        for i in range(2):
            h = h_ref[b * 2 + i]
            o_ref[b * 2 + i] = tn(h, h)


def hgram(h):
    n = h.shape[0]
    return pl.pallas_call(
        hgram_kernel,
        out_shape=jax.ShapeDtypeStruct((n, TOK, TOK), F32),
        in_specs=[VM],
        out_specs=VM,
        compiler_params=limit(8),
        cost_estimate=cost(2 * n * TOK * TOK * BLK, n * TOK * (BLK * 2 + TOK * 4)),
        name="hgram",
    )(h)


def gram_kernel(chunk, s_ref, *refs):
    bufs = (refs[:8], refs[8:16])
    h_ref, before_ref, o_ref, p_ref, g_ref, sems, out_sems = refs[16:]
    z, c = s_ref[0], s_ref[1]
    copies = []
    for u in range(2):
        for k in range(8):
            at = pl.multiple_of(lax.rem(z + 8 - k, 8) * ROWS, ROWS)
            copy = pltpu.make_async_copy(bufs[u][k], g_ref.at[u, :, pl.ds(at, ROWS), :], sems.at[u, k])
            copy.start()
            copies.append(copy)
    lanes = lax.broadcasted_iota(jnp.int32, p_ref.shape, 1)
    p_ref[...] = before_ref[...]
    outs = []
    for u in range(2):
        for k in range(8):
            copies[u * 8 + k].wait()
        out = pltpu.make_async_copy(g_ref.at[u], o_ref.at[u], out_sems.at[u])
        out.start()
        outs.append(out)
        group = c if u == 0 else 1 - c

        @pl.loop(0, 2)
        def _(b):
            m = g_ref[u, pl.ds(b * 2, 2)].reshape(2 * TOK, HALF)
            cot = nt(m, m)
            vec = jnp.zeros(p_ref.shape, F32)
            for i in range(2):
                h = h_ref[u, chunk * 4 + b * 2 + i]
                s = jnp.sum(cot[i * TOK : (i + 1) * TOK, i * TOK : (i + 1) * TOK] * h)
                vec += jnp.where(lanes == group * 8 + chunk * 4 + b * 2 + i, s, 0.0)
            p_ref[...] += vec

    for out in outs:
        out.wait()


def gram(chunk, zc, own, par, hg, before):
    return pl.pallas_call(
        lambda *r: gram_kernel(chunk, *r),
        out_shape=(pltpu.HBM((2, 4, TOK, HALF), BF16), jax.ShapeDtypeStruct((64, TOK), F32)),
        in_specs=[SM] + [ANY] * 16 + [VM, VM],
        out_specs=(HBM, VM),
        scratch_shapes=[
            pltpu.VMEM((2, 4, TOK, HALF), BF16),
            pltpu.SemaphoreType.DMA((2, 8)),
            pltpu.SemaphoreType.DMA((2,)),
        ],
        compiler_params=limit(10),
        cost_estimate=cost(8 * 2 * TOK * 2 * TOK * HALF, 8 * TOK * HALF * 4),
        name="gram",
    )(zc, *own, *par, hg, before)


def fetch(dest, s, ga, gb, gm, gt, sems):
    main = pl.ds(pl.multiple_of(dest * MAIN, MAIN), MAIN)
    last = pl.ds(pl.multiple_of(4 * MAIN + dest // 2 * 128, 128), 128)
    at = (s // 2, pl.ds(s % 2 * 2, 2), slice(None))
    return [
        pltpu.make_async_copy(g.at[(*at, cols)], to.at[s, ch], sems.at[s, ch, j])
        for ch, g in enumerate((ga, gb))
        for j, (cols, to) in enumerate(((main, gm), (last, gt)))
    ]


def accumulate(s, a, gm, gt, acc, tail):
    b = jnp.concatenate([gm[s, ch].reshape(2 * TOK, MAIN) for ch in range(2)], axis=0)
    t = jnp.concatenate([gt[s, ch].reshape(2 * TOK, 128) for ch in range(2)], axis=0)
    acc[...] += nn(a, b)
    tail[...] += nn(a, t)


def finish(dest, acc, tail, box, sem, o_ref):
    box[:, :MAIN] = acc[...].astype(box.dtype)
    v = tail[...]
    v = jnp.where(dest % 2 == 1, pltpu.roll(v, TAIL, 1), v)
    box[:, MAIN:] = v[:, :TAIL].astype(box.dtype)
    copy = pltpu.make_async_copy(box, o_ref, sem)
    copy.start()
    copy.wait()


def first_kernel(radius, s_ref, ga, gb, h_ref, n_ref, o_ref, a_ref, acc, tail, box, sem, *g):
    for s in range(4):
        for copy in fetch(s_ref[0], s, ga, gb, *g):
            copy.start()
    clip = radius / jnp.sqrt(jnp.sum(n_ref[...], axis=0, keepdims=True) + 1e-06)
    lanes = lax.broadcasted_iota(jnp.int32, clip.shape, 1)
    c = s_ref[1]
    acc[...] = jnp.zeros_like(acc)
    tail[...] = jnp.zeros_like(tail)

    @pl.loop(0, 4)
    def _(s):
        u = s // 2
        group = jnp.where(u == 0, c, 1 - c)
        for ch in range(2):
            for i in range(2):
                seq = ch * 4 + s % 2 * 2 + i
                f = jnp.sum(jnp.where(lanes == group * 8 + seq, clip, 0.0))
                j = ch * 2 + i
                a_ref[s, :, j * TOK : (j + 1) * TOK] = (h_ref[u * 8 + seq].astype(F32) * f).astype(BF16)
        for copy in fetch(s_ref[0], s, ga, gb, *g):
            copy.wait()
        accumulate(s, a_ref[s], *g[:2], acc, tail)

    finish(s_ref[0], acc, tail, box, sem, o_ref)


def next_kernel(s_ref, ga, gb, a_ref, o_ref, acc, tail, box, sem, *g):
    for s in range(4):
        for copy in fetch(s_ref[0], s, ga, gb, *g):
            copy.start()
    acc[...] = jnp.zeros_like(acc)
    tail[...] = jnp.zeros_like(tail)

    @pl.loop(0, 4)
    def _(s):
        for copy in fetch(s_ref[0], s, ga, gb, *g):
            copy.wait()
        accumulate(s, a_ref[s], *g[:2], acc, tail)

    finish(s_ref[0], acc, tail, box, sem, o_ref)


def boxes(dtype):
    return [
        pltpu.VMEM((BLK, MAIN), F32),
        pltpu.VMEM((BLK, 128), F32),
        pltpu.VMEM((BLK, BLK), dtype),
        pltpu.SemaphoreType.DMA,
        pltpu.VMEM((4, 2, 2, TOK, MAIN), BF16),
        pltpu.VMEM((4, 2, 2, TOK, 128), BF16),
        pltpu.SemaphoreType.DMA((4, 2, 2)),
    ]


W_COST = cost(2 * 16 * TOK * BLK * 640, 16 * TOK * (640 + BLK) * 2 + BLK * BLK * 4)


def wgrad_first(dest, c, ga, gb, hid, norms, radius):
    return pl.pallas_call(
        lambda *r: first_kernel(radius, *r),
        out_shape=(jax.ShapeDtypeStruct((BLK, BLK), BF16), jax.ShapeDtypeStruct((4, BLK, 4 * TOK), BF16)),
        in_specs=[SM, HBM, HBM, VM, VM],
        out_specs=(ANY, VM),
        scratch_shapes=boxes(BF16),
        compiler_params=limit(12),
        cost_estimate=W_COST,
        name="wgrad_first",
    )(jnp.stack([dest, c]).astype(jnp.int32), ga, gb, hid, norms)


def wgrad_next(dest, ga, gb, a, dtype):
    return pl.pallas_call(
        next_kernel,
        out_shape=jax.ShapeDtypeStruct((BLK, BLK), dtype),
        in_specs=[SM, HBM, HBM, VM],
        out_specs=ANY,
        scratch_shapes=boxes(dtype),
        compiler_params=limit(12),
        cost_estimate=W_COST,
        name="wgrad_next",
    )(dest.reshape(1).astype(jnp.int32), ga, gb, a)


def dhid_kernel(s_ref, ga, gb, w0, w1, w2, w3, wt, o_ref, m_ref, sems):
    def copy(g, j):
        return pltpu.make_async_copy(g.at[s_ref[0], pl.ds(j % 2 * 2, 2)], m_ref.at[j], sems.at[j])

    for j in range(4):
        copy((ga, gb)[j // 2], j).start()

    @pl.loop(0, 4)
    def _(j):
        copy(ga, j).wait()
        total = nt(wt[...], m_ref[j, :, :, 4 * MAIN :].reshape(2 * TOK, 4 * TAIL))
        for k, w in enumerate((w0, w1, w2, w3)):
            cols = pl.ds(pl.multiple_of(lax.rem(s_ref[1] + 4 - k, 4) * MAIN, MAIN), MAIN)
            total += nt(w[:, :MAIN], m_ref[j, :, :, cols].reshape(2 * TOK, MAIN))
        for i in range(2):
            o_ref[j * 2 + i] = total[:, i * TOK : (i + 1) * TOK].astype(o_ref.dtype)


def dhid(ux, g, ws, wt, dtype):
    return pl.pallas_call(
        dhid_kernel,
        out_shape=jax.ShapeDtypeStruct((8, BLK, TOK), dtype),
        in_specs=[SM, HBM, HBM] + [VM] * 5,
        out_specs=VM,
        scratch_shapes=[pltpu.VMEM((4, 2, TOK, HALF), BF16), pltpu.SemaphoreType.DMA((4,))],
        compiler_params=limit(10),
        cost_estimate=cost(2 * 8 * TOK * BLK * HALF, 8 * TOK * HALF * 2 + BLK * HALF * 2),
        name="dhid",
    )(ux, *g, *ws, wt)


def barrier(*xs):
    return lax.optimization_barrier(xs)


def body(hidden, cotangent, w_down, lengths):
    xi, yh, zi, yl, ci = (lax.axis_index(a) for a in ("x", "yh", "z", "yl", "c"))
    seqs, slots, width = cotangent.shape
    units = hidden.shape[2]

    def z_shift(v, k):
        return lax.ppermute(v, "z", [(i, (i + k) % 8) for i in range(8)])

    def x_shift(v, k):
        return lax.ppermute(v, "x", [(i, (i + k) % 4) for i in range(4)])

    def y_swap(v):
        return lax.ppermute(v, "yh", [(0, 1), (1, 0)])

    def c_swap(v):
        return lax.ppermute(v, "c", [(0, 1), (1, 0)])

    pos = ((zi * 2 + yl) * 2 + ci) * slots + jnp.arange(slots, dtype=jnp.int32)
    keep = pos[None, :] < lengths[:, None]
    masked = jnp.where(keep[:, :, None], cotangent, jnp.zeros((), cotangent.dtype))

    def half(h):
        at = [(2 * x + h) * BLK for x in range(4)]
        return jnp.concatenate(
            [masked[:, :, o : o + MAIN] for o in at] + [masked[:, :, o + MAIN : o + BLK] for o in at], axis=2
        )

    h0, h1 = half(0), half(1)
    to_send = (jnp.where(ci == 0, h0, h1), jnp.where(ci == 0, h1, h0))

    got = {}
    for k1 in range(2):
        for k2 in range(2):
            perm = []
            for a in range(2):
                for b in range(2):
                    for c in range(2):
                        perm.append((a * 4 + b * 2 + c, (c ^ k1) * 4 + (b ^ k2) * 2 + a))
            got[k1, k2] = lax.ppermute(to_send[k1], ("yh", "yl", "c"), perm)

    def assemble(lo, hi):
        rows = []
        for q in range(2):
            for p in range(2):
                s0 = jnp.where(yl == 0, got[p, q][lo:hi], got[p, q ^ 1][lo:hi])
                s1 = jnp.where(yl == 0, got[p ^ 1, q][lo:hi], got[p ^ 1, q ^ 1][lo:hi])
                rows.append(jnp.where(yh == 0, s0, s1))
        return jnp.concatenate(rows, axis=1)

    first = [assemble(0, 4), assemble(4, 8)]
    bufs = [[None] * 8 for _ in range(2)]
    for ch in range(2):
        bufs[ch][0] = first[ch]
    fwd, bwd = list(first), list(first)
    for k in range(1, 5):
        for ch in range(2):
            fwd[ch] = z_shift(fwd[ch], 1)
            bufs[ch][k] = fwd[ch]
            if k < 4:
                bwd[ch] = z_shift(bwd[ch], -1)
                bufs[ch][8 - k] = bwd[ch]
    par = [[c_swap(v) for v in bufs[ch]] for ch in range(2)]

    ht, _ = barrier(jnp.swapaxes(hidden, 1, 2), first[1])
    other = y_swap(ht)
    same = yh == ci
    hid = jnp.concatenate([jnp.where(same, ht, other), jnp.where(same, other, ht)], axis=0)
    hg = hgram(hid).reshape(2, 8, TOK, TOK)

    w_own, _ = barrier(w_down, first[1])
    ws = [w_own]
    for k in range(1, 4):
        ws.append(x_shift(w_own, k))
    tails = [w[:, MAIN:] for w in ws]
    nat = []
    for x in range(4):
        v = tails[(0 - x) % 4]
        for me in (1, 2, 3):
            v = jnp.where(xi == me, tails[(me - x) % 4], v)
        nat.append(v)
    wt = jnp.concatenate(nat, axis=1)

    zc = jnp.stack([zi, ci]).astype(jnp.int32)
    part, wt = barrier(jnp.zeros((64, TOK), F32), wt)
    g = [None, None]
    for ch in range(2):
        g[ch], part = gram(ch, zc, bufs[ch], par[ch], hg, part)
    g = [pltpu.with_memory_space_constraint(v, pltpu.HBM) for v in g]
    norms = lax.all_to_all(part, ("yh", "z", "yl", "c"), 0, 0, tiled=True)
    radius = math.sqrt(units * 32 * width / (seqs * 8))

    pieces = {}
    pieces[2], a = wgrad_first(lax.rem(xi + 2, 4), ci, g[0], g[1], hid, norms, radius)
    for k in (1, 3):
        pieces[k] = wgrad_next(lax.rem(xi + k, 4), g[0], g[1], a, BF16)
    weight_grad = wgrad_next(xi, g[0], g[1], a, F32)
    for k in (2, 1, 3):
        v = x_shift(pieces[k], k)
        weight_grad = weight_grad + v.astype(F32)

    mine = jnp.where(same, 0, 1)
    theirs = dhid(jnp.stack([1 - mine, xi]).astype(jnp.int32), g, ws, wt, BF16)
    theirs = y_swap(theirs)
    ours = dhid(jnp.stack([mine, xi]).astype(jnp.int32), g, ws, wt, F32)
    d_hidden = (ours + theirs.astype(F32)).astype(BF16)
    return weight_grad, jnp.swapaxes(d_hidden, 1, 2)


def solution(mesh):
    fine = Mesh(mesh.devices.reshape(4, 2, 8, 2, 2), ("x", "yh", "z", "yl", "c"))
    dp, mp = ("x", "yh"), ("z", "yl", "c")
    in_specs = (P(dp, None, mp), P(dp, mp, None), P(mp, dp), P(dp))
    out_specs = (P(mp, dp), P(dp, None, mp))

    return jax.shard_map(body, mesh=fine, in_specs=in_specs, out_specs=out_specs, check_vma=False)
```

```python
import math

import jax
import jax.numpy as jnp
from jax import lax
from jax.experimental import pallas as pl
from jax.experimental.pallas import tpu as pltpu
from jax.sharding import Mesh
from jax.sharding import PartitionSpec as P


TOK = 128
BLK = 576
MAIN = 512
TAIL = BLK - MAIN
HALF = 4 * BLK
ROWS = 16
F32 = jnp.float32
BF16 = jnp.bfloat16


def nt(a, b):
    return lax.dot_general(a, b, (((1,), (1,)), ((), ())), preferred_element_type=F32)


def tn(a, b):
    return lax.dot_general(a, b, (((0,), (0,)), ((), ())), preferred_element_type=F32)


def nn(a, b):
    return lax.dot_general(a, b, (((1,), (0,)), ((), ())), preferred_element_type=F32)


def cost(flops, moved):
    return pl.CostEstimate(flops=int(flops), bytes_accessed=int(moved), transcendentals=0)


VM = pl.BlockSpec(memory_space=pltpu.VMEM)
ANY = pl.BlockSpec(memory_space=pl.ANY)
HBM = pl.BlockSpec(memory_space=pltpu.HBM)
SM = pl.BlockSpec(memory_space=pltpu.SMEM)


def limit(mib):
    return pltpu.CompilerParams(vmem_limit_bytes=mib * 2**20)


def hgram_kernel(h_ref, o_ref, box, sem):
    @pl.loop(0, h_ref.shape[0] // 2)
    def _(b):
        for i in range(2):
            h = h_ref[b * 2 + i]
            box[b * 2 + i] = tn(h, h)

    copy = pltpu.make_async_copy(box, o_ref, sem)
    copy.start()
    copy.wait()


def hgram(h):
    n = h.shape[0]
    return pl.pallas_call(
        hgram_kernel,
        out_shape=pltpu.HBM((n, TOK, TOK), F32),
        in_specs=[VM],
        out_specs=HBM,
        scratch_shapes=[pltpu.VMEM((n, TOK, TOK), F32), pltpu.SemaphoreType.DMA],
        compiler_params=limit(10),
        cost_estimate=cost(2 * n * TOK * TOK * BLK, n * TOK * (BLK * 2 + TOK * 4)),
        name="hgram",
    )(h)


def gram_kernel(chunk, s_ref, *refs):
    bufs = (refs[:8], refs[8:16])
    h_hbm, before_ref, o_ref, p_ref, g_ref, h_ref, sems, out_sems, h_sem = refs[16:]
    z, c = s_ref[0], s_ref[1]
    for u in range(2):
        for k in range(8):
            at = pl.multiple_of(lax.rem(z + 8 - k, 8) * ROWS, ROWS)
            buf = bufs[u][k].at[pl.ds(chunk * 4, 4)] if (u, k) == (1, 0) else bufs[u][k]
            pltpu.make_async_copy(buf, g_ref.at[u, :, pl.ds(at, ROWS), :], sems.at[u, k]).start()
        if u == 0:
            hid = pltpu.make_async_copy(h_hbm.at[:, pl.ds(chunk * 4, 4)], h_ref, h_sem)
            hid.start()
    lanes = lax.broadcasted_iota(jnp.int32, p_ref.shape, 1)
    p_ref[...] = before_ref[...]

    def out(u):
        return pltpu.make_async_copy(g_ref.at[u], o_ref.at[u], out_sems.at[u])

    @pl.loop(0, 4)
    def _(j):
        u, b = j // 2, j % 2

        @pl.when(b == 0)
        def _():
            for k in range(8):
                at = pl.multiple_of(lax.rem(z + 8 - k, 8) * ROWS, ROWS)
                pltpu.make_async_copy(bufs[0][k], g_ref.at[u, :, pl.ds(at, ROWS), :], sems.at[u, k]).wait()
            out(u).start()

        @pl.when(j == 0)
        def _():
            hid.wait()

        m = g_ref[u, pl.ds(b * 2, 2)].reshape(2 * TOK, HALF)
        cot = nt(m, m)
        group = jnp.where(u == 0, c, 1 - c)
        vec = jnp.zeros(p_ref.shape, F32)
        for i in range(2):
            h = h_ref[u, b * 2 + i]
            s = jnp.sum(cot[i * TOK : (i + 1) * TOK, i * TOK : (i + 1) * TOK] * h)
            vec += jnp.where(lanes == group * 8 + chunk * 4 + b * 2 + i, s, 0.0)
        p_ref[...] += vec

    for u in range(2):
        out(u).wait()


def gram(chunk, zc, own, par, hg, before):
    return pl.pallas_call(
        lambda *r: gram_kernel(chunk, *r),
        out_shape=(pltpu.HBM((2, 4, TOK, HALF), BF16), jax.ShapeDtypeStruct((64, TOK), F32)),
        in_specs=[SM] + [ANY] * 16 + [HBM, VM],
        out_specs=(HBM, VM),
        scratch_shapes=[
            pltpu.VMEM((2, 4, TOK, HALF), BF16),
            pltpu.VMEM((2, 4, TOK, TOK), F32),
            pltpu.SemaphoreType.DMA((2, 8)),
            pltpu.SemaphoreType.DMA((2,)),
            pltpu.SemaphoreType.DMA,
        ],
        compiler_params=limit(14),
        cost_estimate=cost(8 * 2 * TOK * 2 * TOK * HALF, 8 * TOK * HALF * 4),
        name="gram",
    )(zc, *own, *par, hg, before)


def fetch(dest, s, ga, gb, gm, gt, sems):
    main = pl.ds(pl.multiple_of(dest * MAIN, MAIN), MAIN)
    last = pl.ds(pl.multiple_of(4 * MAIN + dest // 2 * 128, 128), 128)
    at = (s // 2, pl.ds(s % 2 * 2, 2), slice(None))
    return [
        pltpu.make_async_copy(g.at[(*at, cols)], to.at[s, ch], sems.at[s, ch, j])
        for ch, g in enumerate((ga, gb))
        for j, (cols, to) in enumerate(((main, gm), (last, gt)))
    ]


def accumulate(s, a, gm, gt, acc, tail):
    b = jnp.concatenate([gm[s, ch].reshape(2 * TOK, MAIN) for ch in range(2)], axis=0)
    t = jnp.concatenate([gt[s, ch].reshape(2 * TOK, 128) for ch in range(2)], axis=0)
    acc[...] += nn(a, b)
    tail[...] += nn(a, t)


def finish(dest, acc, tail, box, sem, outs, d):
    box[:, :MAIN] = acc[...].astype(box.dtype)
    v = tail[...]
    v = jnp.where(dest % 2 == 1, pltpu.roll(v, TAIL, 1), v)
    box[:, MAIN:] = v[:, :TAIL].astype(box.dtype)
    for i, o_ref in enumerate(outs):

        @pl.when(d == i)
        def _():
            pltpu.make_async_copy(box, o_ref, sem).start()

    pltpu.make_async_copy(box, outs[0], sem).wait()


def first_kernel(radius, s_ref, ga, gb, h_ref, n_ref, o_ref, a_ref, acc, tail, box, sem, *g):
    for s in range(4):
        for copy in fetch(s_ref[0], s, ga, gb, *g):
            copy.start()
    clip = radius / jnp.sqrt(jnp.sum(n_ref[...], axis=0, keepdims=True) + 1e-06)
    lanes = lax.broadcasted_iota(jnp.int32, clip.shape, 1)
    c = s_ref[1]
    acc[...] = jnp.zeros_like(acc)
    tail[...] = jnp.zeros_like(tail)

    @pl.loop(0, 4)
    def _(s):
        u = s // 2
        group = jnp.where(u == 0, c, 1 - c)
        for ch in range(2):
            for i in range(2):
                seq = ch * 4 + s % 2 * 2 + i
                f = jnp.sum(jnp.where(lanes == group * 8 + seq, clip, 0.0))
                j = ch * 2 + i
                a_ref[s, :, j * TOK : (j + 1) * TOK] = (h_ref[u * 8 + seq].astype(F32) * f).astype(BF16)
        for copy in fetch(s_ref[0], s, ga, gb, *g):
            copy.wait()
        accumulate(s, a_ref[s], *g[:2], acc, tail)

    finish(s_ref[0], acc, tail, box, sem, [o_ref], 0)


def next_kernel(s_ref, ga, gb, a_ref, *refs):
    n = len(refs) - 7
    outs, (acc, tail, box, sem, *g) = refs[:n], refs[n:]

    @pl.loop(0, n)
    def _(d):
        for s in range(4):
            for copy in fetch(s_ref[d], s, ga, gb, *g):
                copy.start()
        acc[...] = jnp.zeros_like(acc)
        tail[...] = jnp.zeros_like(tail)

        @pl.loop(0, 4)
        def _(s):
            for copy in fetch(s_ref[d], s, ga, gb, *g):
                copy.wait()
            accumulate(s, a_ref[s], *g[:2], acc, tail)

        finish(s_ref[d], acc, tail, box, sem, outs, d)


def boxes(dtype):
    return [
        pltpu.VMEM((BLK, MAIN), F32),
        pltpu.VMEM((BLK, 128), F32),
        pltpu.VMEM((BLK, BLK), dtype),
        pltpu.SemaphoreType.DMA,
        pltpu.VMEM((4, 2, 2, TOK, MAIN), BF16),
        pltpu.VMEM((4, 2, 2, TOK, 128), BF16),
        pltpu.SemaphoreType.DMA((4, 2, 2)),
    ]


W_COST = cost(2 * 16 * TOK * BLK * 640, 16 * TOK * (640 + BLK) * 2 + BLK * BLK * 4)


def wgrad_first(dest, c, ga, gb, hid, norms, radius):
    return pl.pallas_call(
        lambda *r: first_kernel(radius, *r),
        out_shape=(jax.ShapeDtypeStruct((BLK, BLK), BF16), jax.ShapeDtypeStruct((4, BLK, 4 * TOK), BF16)),
        in_specs=[SM, HBM, HBM, VM, VM],
        out_specs=(ANY, VM),
        scratch_shapes=boxes(BF16),
        compiler_params=limit(14),
        cost_estimate=W_COST,
        name="wgrad_first",
    )(jnp.stack([dest, c]).astype(jnp.int32), ga, gb, hid, norms)


def wgrad_next(dests, ga, gb, a, dtype):
    n = len(dests)
    return pl.pallas_call(
        next_kernel,
        out_shape=[jax.ShapeDtypeStruct((BLK, BLK), dtype)] * n,
        in_specs=[SM, HBM, HBM, VM],
        out_specs=[ANY] * n,
        scratch_shapes=boxes(dtype),
        compiler_params=limit(14),
        cost_estimate=cost(n * W_COST.flops, n * W_COST.bytes_accessed),
        name="wgrad_next",
    )(jnp.stack(dests).astype(jnp.int32), ga, gb, a)


def dhid_kernel(s_ref, ga, gb, w0, w1, w2, w3, wt, *refs):
    *more, o_ref, m_ref, sems = refs

    def copy(g, j):
        return pltpu.make_async_copy(g.at[s_ref[0], pl.ds(j % 2 * 2, 2)], m_ref.at[j], sems.at[j])

    for j in range(4):
        copy((ga, gb)[j // 2], j).start()

    @pl.loop(0, 4)
    def _(j):
        copy(ga, j).wait()
        total = nt(wt[...], m_ref[j, :, :, 4 * MAIN :].reshape(2 * TOK, 4 * TAIL))
        for k, w in enumerate((w0, w1, w2, w3)):
            cols = pl.ds(pl.multiple_of(lax.rem(s_ref[1] + 4 - k, 4) * MAIN, MAIN), MAIN)
            total += nt(w[:, :MAIN], m_ref[j, :, :, cols].reshape(2 * TOK, MAIN))
        for i in range(2):
            v = total[:, i * TOK : (i + 1) * TOK]
            if more:
                v += more[0][j * 2 + i].astype(F32)
            o_ref[j * 2 + i] = v.astype(o_ref.dtype)


def dhid(ux, g, ws, wt, *more):
    return pl.pallas_call(
        dhid_kernel,
        out_shape=jax.ShapeDtypeStruct((8, BLK, TOK), BF16),
        in_specs=[SM, HBM, HBM] + [VM] * (5 + len(more)),
        out_specs=VM,
        scratch_shapes=[pltpu.VMEM((4, 2, TOK, HALF), BF16), pltpu.SemaphoreType.DMA((4,))],
        compiler_params=limit(14),
        cost_estimate=cost(2 * 8 * TOK * BLK * HALF, 8 * TOK * HALF * 2 + BLK * HALF * 2),
        name="dhid",
    )(ux, *g, *ws, wt, *more)


def barrier(*xs):
    return lax.optimization_barrier(xs)


def body(hidden, cotangent, w_down, lengths):
    xi, yh, zi, yl, ci = (lax.axis_index(a) for a in ("x", "yh", "z", "yl", "c"))
    seqs, slots, width = cotangent.shape
    units = hidden.shape[2]

    def z_shift(v, k):
        return lax.ppermute(v, "z", [(i, (i + k) % 8) for i in range(8)])

    def x_shift(v, k):
        return lax.ppermute(v, "x", [(i, (i + k) % 4) for i in range(4)])

    def y_swap(v):
        return lax.ppermute(v, "yh", [(0, 1), (1, 0)])

    def c_swap(v):
        return lax.ppermute(v, "c", [(0, 1), (1, 0)])

    pos = ((zi * 2 + yl) * 2 + ci) * slots + jnp.arange(slots, dtype=jnp.int32)
    keep = pos[None, :] < lengths[:, None]
    masked = jnp.where(keep[:, :, None], cotangent, jnp.zeros((), cotangent.dtype))

    def half(h):
        at = [(2 * x + h) * BLK for x in range(4)]
        return jnp.concatenate(
            [masked[:, :, o : o + MAIN] for o in at] + [masked[:, :, o + MAIN : o + BLK] for o in at], axis=2
        )

    h0, h1 = half(0), half(1)
    to_send = (jnp.where(ci == 0, h0, h1), jnp.where(ci == 0, h1, h0))

    got = {}
    for k1 in range(2):
        for k2 in range(2):
            perm = []
            for a in range(2):
                for b in range(2):
                    for c in range(2):
                        perm.append((a * 4 + b * 2 + c, (c ^ k1) * 4 + (b ^ k2) * 2 + a))
            got[k1, k2] = lax.ppermute(to_send[k1], ("yh", "yl", "c"), perm)

    def assemble(lo, hi):
        rows = []
        for q in range(2):
            for p in range(2):
                s0 = jnp.where(yl == 0, got[p, q][lo:hi], got[p, q ^ 1][lo:hi])
                s1 = jnp.where(yl == 0, got[p ^ 1, q][lo:hi], got[p ^ 1, q ^ 1][lo:hi])
                rows.append(jnp.where(yh == 0, s0, s1))
        return jnp.concatenate(rows, axis=1)

    first = [assemble(0, 4), assemble(4, 8)]
    bufs = [[None] * 8 for _ in range(2)]
    for ch in range(2):
        bufs[ch][0] = first[ch]
    fwd, bwd = list(first), list(first)
    for k in range(1, 5):
        for ch in range(2):
            fwd[ch] = z_shift(fwd[ch], 1)
            bufs[ch][k] = fwd[ch]
            if k < 4:
                bwd[ch] = z_shift(bwd[ch], -1)
                bufs[ch][8 - k] = bwd[ch]
    par = [[None] * 8 for _ in range(2)]
    par[0][0] = par[1][0] = c_swap(jnp.concatenate(first, axis=0))
    for ch in range(2):
        for k in range(1, 8):
            par[ch][k] = c_swap(bufs[ch][k])

    ht, _ = barrier(jnp.swapaxes(hidden, 1, 2), first[1])
    other = y_swap(ht)
    same = yh == ci
    hid = jnp.concatenate([jnp.where(same, ht, other), jnp.where(same, other, ht)], axis=0)
    hg = hgram(hid).reshape(2, 8, TOK, TOK)
    hg = pltpu.with_memory_space_constraint(hg, pltpu.HBM)

    w_own, _ = barrier(w_down, first[1])
    ws = [w_own]
    for k in range(1, 4):
        ws.append(x_shift(w_own, k))
    zc = jnp.stack([zi, ci]).astype(jnp.int32)
    part = jnp.zeros((64, TOK), F32)
    g = [None, None]
    for ch in range(2):
        g[ch], part = gram(ch, zc, bufs[ch], par[ch], hg, part)
    g = [pltpu.with_memory_space_constraint(v, pltpu.HBM) for v in g]
    norms = lax.all_to_all(part, ("yh", "z", "yl", "c"), 0, 0, tiled=True)
    *ws, _ = barrier(*ws, part)
    tails = [w[:, MAIN:] for w in ws]
    nat = []
    for x in range(4):
        v = tails[(0 - x) % 4]
        for me in (1, 2, 3):
            v = jnp.where(xi == me, tails[(me - x) % 4], v)
        nat.append(v)
    wt = jnp.concatenate(nat, axis=1)
    radius = math.sqrt(units * 32 * width / (seqs * 8))

    pieces = {}
    pieces[2], a = wgrad_first(lax.rem(xi + 2, 4), ci, g[0], g[1], hid, norms, radius)
    pieces[1], pieces[3] = wgrad_next([lax.rem(xi + k, 4) for k in (1, 3)], g[0], g[1], a, BF16)
    (weight_grad,) = wgrad_next([xi], g[0], g[1], a, F32)
    for k in (2, 1, 3):
        v = x_shift(pieces[k], k)
        weight_grad = weight_grad + v.astype(F32)

    mine = jnp.where(same, 0, 1)
    theirs = dhid(jnp.stack([1 - mine, xi]).astype(jnp.int32), g, ws, wt)
    theirs = y_swap(theirs)
    d_hidden = dhid(jnp.stack([mine, xi]).astype(jnp.int32), g, ws, wt, theirs)
    return weight_grad, jnp.swapaxes(d_hidden, 1, 2)


def solution(mesh):
    fine = Mesh(mesh.devices.reshape(4, 2, 8, 2, 2), ("x", "yh", "z", "yl", "c"))
    dp, mp = ("x", "yh"), ("z", "yl", "c")
    in_specs = (P(dp, None, mp), P(dp, mp, None), P(mp, dp), P(dp))
    out_specs = (P(mp, dp), P(dp, None, mp))

    return jax.shard_map(body, mesh=fine, in_specs=in_specs, out_specs=out_specs, check_vma=False)
```

```python
import math

import jax
import jax.numpy as jnp
from jax import lax
from jax.experimental import pallas as pl
from jax.experimental.pallas import tpu as pltpu
from jax.sharding import Mesh
from jax.sharding import PartitionSpec as P


TOK = 128
BLK = 576
MAIN = 512
TAIL = BLK - MAIN
HALF = 4 * BLK
SLAB = BLK // 8
ROWS = 16
F32 = jnp.float32
BF16 = jnp.bfloat16


def nt(a, b):
    return lax.dot_general(a, b, (((1,), (1,)), ((), ())), preferred_element_type=F32)


def tn(a, b):
    return lax.dot_general(a, b, (((0,), (0,)), ((), ())), preferred_element_type=F32)


def nn(a, b):
    return lax.dot_general(a, b, (((1,), (0,)), ((), ())), preferred_element_type=F32)


def cost(flops, moved):
    return pl.CostEstimate(flops=int(flops), bytes_accessed=int(moved), transcendentals=0)


VM = pl.BlockSpec(memory_space=pltpu.VMEM)
ANY = pl.BlockSpec(memory_space=pl.ANY)
HBM = pl.BlockSpec(memory_space=pltpu.HBM)
SM = pl.BlockSpec(memory_space=pltpu.SMEM)


def limit(mib):
    return pltpu.CompilerParams(vmem_limit_bytes=mib * 2**20)


def hgram_kernel(h_ref, o_ref, box, sem):
    @pl.loop(0, h_ref.shape[0] // 2)
    def _(b):
        for i in range(2):
            h = h_ref[b * 2 + i]
            box[b * 2 + i] = tn(h, h)

    copy = pltpu.make_async_copy(box, o_ref, sem)
    copy.start()
    copy.wait()


def hgram(h):
    n = h.shape[0]
    return pl.pallas_call(
        hgram_kernel,
        out_shape=pltpu.HBM((n, TOK, TOK), F32),
        in_specs=[VM],
        out_specs=HBM,
        scratch_shapes=[pltpu.VMEM((n, TOK, TOK), F32), pltpu.SemaphoreType.DMA],
        compiler_params=limit(10),
        cost_estimate=cost(2 * n * TOK * TOK * BLK, n * TOK * (BLK * 2 + TOK * 4)),
        name="hgram",
    )(h)


def gram_kernel(chunk, s_ref, *refs):
    bufs = (refs[:8], refs[8:16])
    h_hbm, before_ref, o_ref, p_ref, g_ref, h_ref, sems, out_sems, h_sem = refs[16:]
    z, c = s_ref[0], s_ref[1]
    for u in range(2):
        for k in range(8):
            at = pl.multiple_of(lax.rem(z + 8 - k, 8) * ROWS, ROWS)
            buf = bufs[u][k].at[pl.ds(chunk * 4, 4)] if (u, k) == (1, 0) else bufs[u][k]
            pltpu.make_async_copy(buf, g_ref.at[u, :, pl.ds(at, ROWS), :], sems.at[u, k]).start()
        if u == 0:
            hid = pltpu.make_async_copy(h_hbm.at[:, pl.ds(chunk * 4, 4)], h_ref, h_sem)
            hid.start()
    lanes = lax.broadcasted_iota(jnp.int32, p_ref.shape, 1)
    p_ref[...] = before_ref[...]

    def out(u):
        return pltpu.make_async_copy(g_ref.at[u], o_ref.at[u], out_sems.at[u])

    @pl.loop(0, 4)
    def _(j):
        u, b = j // 2, j % 2

        @pl.when(b == 0)
        def _():
            for k in range(8):
                at = pl.multiple_of(lax.rem(z + 8 - k, 8) * ROWS, ROWS)
                pltpu.make_async_copy(bufs[0][k], g_ref.at[u, :, pl.ds(at, ROWS), :], sems.at[u, k]).wait()
            out(u).start()

        @pl.when(j == 0)
        def _():
            hid.wait()

        m = g_ref[u, pl.ds(b * 2, 2)].reshape(2 * TOK, HALF)
        cot = nt(m, m)
        group = jnp.where(u == 0, c, 1 - c)
        vec = jnp.zeros(p_ref.shape, F32)
        for i in range(2):
            h = h_ref[u, b * 2 + i]
            s = jnp.sum(cot[i * TOK : (i + 1) * TOK, i * TOK : (i + 1) * TOK] * h)
            vec += jnp.where(lanes == group * 8 + chunk * 4 + b * 2 + i, s, 0.0)
        p_ref[...] += vec

    for u in range(2):
        out(u).wait()


def gram(chunk, zc, own, par, hg, before):
    return pl.pallas_call(
        lambda *r: gram_kernel(chunk, *r),
        out_shape=(pltpu.HBM((2, 4, TOK, HALF), BF16), jax.ShapeDtypeStruct((64, TOK), F32)),
        in_specs=[SM] + [ANY] * 16 + [HBM, VM],
        out_specs=(HBM, VM),
        scratch_shapes=[
            pltpu.VMEM((2, 4, TOK, HALF), BF16),
            pltpu.VMEM((2, 4, TOK, TOK), F32),
            pltpu.SemaphoreType.DMA((2, 8)),
            pltpu.SemaphoreType.DMA((2,)),
            pltpu.SemaphoreType.DMA,
        ],
        compiler_params=limit(14),
        cost_estimate=cost(8 * 2 * TOK * 2 * TOK * HALF, 8 * TOK * HALF * 4),
        name="gram",
    )(zc, *own, *par, hg, before)


def fetch(dest, s, ga, gb, gm, gt, sems):
    main = pl.ds(pl.multiple_of(dest * MAIN, MAIN), MAIN)
    last = pl.ds(pl.multiple_of(4 * MAIN + dest // 2 * 128, 128), 128)
    at = (s // 2, pl.ds(s % 2 * 2, 2), slice(None))
    return [
        pltpu.make_async_copy(g.at[(*at, cols)], to.at[s, ch], sems.at[s, ch, j])
        for ch, g in enumerate((ga, gb))
        for j, (cols, to) in enumerate(((main, gm), (last, gt)))
    ]


def accumulate(s, a, gm, gt, acc, tail):
    b = jnp.concatenate([gm[s, ch].reshape(2 * TOK, MAIN) for ch in range(2)], axis=0)
    t = jnp.concatenate([gt[s, ch].reshape(2 * TOK, 128) for ch in range(2)], axis=0)
    acc[...] += nn(a, b)
    tail[...] += nn(a, t)


def finish(dest, acc, tail, box, sem, outs, d):
    box[:BLK, :] = acc[...].astype(box.dtype)
    v = tail[...]
    v = jnp.where(dest % 2 == 1, pltpu.roll(v, TAIL, 1), v)
    low, high = v[: BLK // 2], pltpu.roll(v[BLK // 2 :], TAIL, 1)
    pair = jnp.where(lax.broadcasted_iota(jnp.int32, low.shape, 1) < TAIL, low, high)
    for j in range(4):
        box[BLK:, j * 128 : (j + 1) * 128] = pair[j * SLAB : (j + 1) * SLAB].astype(box.dtype)
    for i, o_ref in enumerate(outs):

        @pl.when(d == i)
        def _():
            pltpu.make_async_copy(box, o_ref, sem).start()

    pltpu.make_async_copy(box, outs[0], sem).wait()


def first_kernel(radius, s_ref, ga, gb, h_ref, n_ref, o_ref, a_ref, acc, tail, box, sem, *g):
    for s in range(4):
        for copy in fetch(s_ref[0], s, ga, gb, *g):
            copy.start()
    clip = radius / jnp.sqrt(jnp.sum(n_ref[...], axis=0, keepdims=True) + 1e-06)
    lanes = lax.broadcasted_iota(jnp.int32, clip.shape, 1)
    c = s_ref[1]
    acc[...] = jnp.zeros_like(acc)
    tail[...] = jnp.zeros_like(tail)

    @pl.loop(0, 4)
    def _(s):
        u = s // 2
        group = jnp.where(u == 0, c, 1 - c)
        for ch in range(2):
            for i in range(2):
                seq = ch * 4 + s % 2 * 2 + i
                f = jnp.sum(jnp.where(lanes == group * 8 + seq, clip, 0.0))
                j = ch * 2 + i
                a_ref[s, :, j * TOK : (j + 1) * TOK] = (h_ref[u * 8 + seq].astype(F32) * f).astype(BF16)
        for copy in fetch(s_ref[0], s, ga, gb, *g):
            copy.wait()
        accumulate(s, a_ref[s], *g[:2], acc, tail)

    finish(s_ref[0], acc, tail, box, sem, [o_ref], 0)


def next_kernel(s_ref, ga, gb, a_ref, *refs):
    n = len(refs) - 7
    outs, (acc, tail, box, sem, *g) = refs[:n], refs[n:]

    @pl.loop(0, n)
    def _(d):
        for s in range(4):
            for copy in fetch(s_ref[d], s, ga, gb, *g):
                copy.start()
        acc[...] = jnp.zeros_like(acc)
        tail[...] = jnp.zeros_like(tail)

        @pl.loop(0, 4)
        def _(s):
            for copy in fetch(s_ref[d], s, ga, gb, *g):
                copy.wait()
            accumulate(s, a_ref[s], *g[:2], acc, tail)

        finish(s_ref[d], acc, tail, box, sem, outs, d)


def boxes(dtype):
    return [
        pltpu.VMEM((BLK, MAIN), F32),
        pltpu.VMEM((BLK, 128), F32),
        pltpu.VMEM((BLK + SLAB, MAIN), dtype),
        pltpu.SemaphoreType.DMA,
        pltpu.VMEM((4, 2, 2, TOK, MAIN), BF16),
        pltpu.VMEM((4, 2, 2, TOK, 128), BF16),
        pltpu.SemaphoreType.DMA((4, 2, 2)),
    ]


W_COST = cost(2 * 16 * TOK * BLK * 640, 16 * TOK * (640 + BLK) * 2 + BLK * BLK * 4)


def wgrad_first(dest, c, ga, gb, hid, norms, radius):
    return pl.pallas_call(
        lambda *r: first_kernel(radius, *r),
        out_shape=(jax.ShapeDtypeStruct((BLK + SLAB, MAIN), BF16), jax.ShapeDtypeStruct((4, BLK, 4 * TOK), BF16)),
        in_specs=[SM, HBM, HBM, VM, VM],
        out_specs=(ANY, VM),
        scratch_shapes=boxes(BF16),
        compiler_params=limit(14),
        cost_estimate=W_COST,
        name="wgrad_first",
    )(jnp.stack([dest, c]).astype(jnp.int32), ga, gb, hid, norms)


def wgrad_next(dests, ga, gb, a, dtype):
    n = len(dests)
    return pl.pallas_call(
        next_kernel,
        out_shape=[jax.ShapeDtypeStruct((BLK + SLAB, MAIN), dtype)] * n,
        in_specs=[SM, HBM, HBM, VM],
        out_specs=[ANY] * n,
        scratch_shapes=boxes(dtype),
        compiler_params=limit(14),
        cost_estimate=cost(n * W_COST.flops, n * W_COST.bytes_accessed),
        name="wgrad_next",
    )(jnp.stack(dests).astype(jnp.int32), ga, gb, a)


def total_kernel(*refs):
    *ins, o_ref = refs
    for part in range(2):
        o_ref[part, :, :MAIN] = sum(ins[3 * i + part][...].astype(F32) for i in range(4))
    t = sum(ins[3 * i + 2][...].astype(F32) for i in range(4))
    o_ref[0, :, MAIN:] = t[:, :TAIL]
    o_ref[1, :, MAIN:] = pltpu.roll(t, TAIL, 1)[:, :TAIL]


def total(pieces):
    specs = [
        pl.BlockSpec((SLAB, MAIN), lambda j: (j, 0)),
        pl.BlockSpec((SLAB, MAIN), lambda j: (4 + j, 0)),
        pl.BlockSpec((SLAB, 128), lambda j: (8, j)),
    ]
    out = pl.pallas_call(
        total_kernel,
        out_shape=jax.ShapeDtypeStruct((2, BLK // 2, BLK), F32),
        grid=(4,),
        in_specs=specs * 4,
        out_specs=pl.BlockSpec((2, SLAB, BLK), lambda j: (0, j, 0)),
        compiler_params=limit(10),
        cost_estimate=cost(4 * BLK * BLK, 14 * BLK * BLK),
        name="total",
    )(*(p for p in pieces for _ in range(3)))
    return out.reshape(BLK, BLK)


def dhid_kernel(s_ref, ga, gb, w0, w1, w2, w3, wt, *refs):
    *more, o_ref, m_ref, sems = refs

    def copy(g, j):
        return pltpu.make_async_copy(g.at[s_ref[0], pl.ds(j % 2 * 2, 2)], m_ref.at[j], sems.at[j])

    for j in range(4):
        copy((ga, gb)[j // 2], j).start()

    @pl.loop(0, 4)
    def _(j):
        copy(ga, j).wait()
        total = nt(wt[...], m_ref[j, :, :, 4 * MAIN :].reshape(2 * TOK, 4 * TAIL))
        for k, w in enumerate((w0, w1, w2, w3)):
            cols = pl.ds(pl.multiple_of(lax.rem(s_ref[1] + 4 - k, 4) * MAIN, MAIN), MAIN)
            total += nt(w[:, :MAIN], m_ref[j, :, :, cols].reshape(2 * TOK, MAIN))
        for i in range(2):
            v = total[:, i * TOK : (i + 1) * TOK]
            if more:
                v += more[0][j * 2 + i].astype(F32)
            o_ref[j * 2 + i] = v.astype(o_ref.dtype)


def dhid(ux, g, ws, wt, *more):
    return pl.pallas_call(
        dhid_kernel,
        out_shape=jax.ShapeDtypeStruct((8, BLK, TOK), BF16),
        in_specs=[SM, HBM, HBM] + [VM] * (5 + len(more)),
        out_specs=VM,
        scratch_shapes=[pltpu.VMEM((4, 2, TOK, HALF), BF16), pltpu.SemaphoreType.DMA((4,))],
        compiler_params=limit(14),
        cost_estimate=cost(2 * 8 * TOK * BLK * HALF, 8 * TOK * HALF * 2 + BLK * HALF * 2),
        name="dhid",
    )(ux, *g, *ws, wt, *more)


def barrier(*xs):
    return lax.optimization_barrier(xs)


def body(hidden, cotangent, w_down, lengths):
    xi, yh, zi, yl, ci = (lax.axis_index(a) for a in ("x", "yh", "z", "yl", "c"))
    seqs, slots, width = cotangent.shape
    units = hidden.shape[2]

    def z_shift(v, k):
        return lax.ppermute(v, "z", [(i, (i + k) % 8) for i in range(8)])

    def x_shift(v, k):
        return lax.ppermute(v, "x", [(i, (i + k) % 4) for i in range(4)])

    def y_swap(v):
        return lax.ppermute(v, "yh", [(0, 1), (1, 0)])

    def c_swap(v):
        return lax.ppermute(v, "c", [(0, 1), (1, 0)])

    pos = ((zi * 2 + yl) * 2 + ci) * slots + jnp.arange(slots, dtype=jnp.int32)
    keep = pos[None, :] < lengths[:, None]
    masked = jnp.where(keep[:, :, None], cotangent, jnp.zeros((), cotangent.dtype))

    def half(h):
        at = [(2 * x + h) * BLK for x in range(4)]
        return jnp.concatenate(
            [masked[:, :, o : o + MAIN] for o in at] + [masked[:, :, o + MAIN : o + BLK] for o in at], axis=2
        )

    h0, h1 = half(0), half(1)
    to_send = (jnp.where(ci == 0, h0, h1), jnp.where(ci == 0, h1, h0))

    got = {}
    for k1 in range(2):
        for k2 in range(2):
            perm = []
            for a in range(2):
                for b in range(2):
                    for c in range(2):
                        perm.append((a * 4 + b * 2 + c, (c ^ k1) * 4 + (b ^ k2) * 2 + a))
            got[k1, k2] = lax.ppermute(to_send[k1], ("yh", "yl", "c"), perm)

    def assemble(lo, hi):
        rows = []
        for q in range(2):
            for p in range(2):
                s0 = jnp.where(yl == 0, got[p, q][lo:hi], got[p, q ^ 1][lo:hi])
                s1 = jnp.where(yl == 0, got[p ^ 1, q][lo:hi], got[p ^ 1, q ^ 1][lo:hi])
                rows.append(jnp.where(yh == 0, s0, s1))
        return jnp.concatenate(rows, axis=1)

    first = [assemble(0, 4), assemble(4, 8)]
    bufs = [[None] * 8 for _ in range(2)]
    for ch in range(2):
        bufs[ch][0] = first[ch]
    fwd, bwd = list(first), list(first)
    for k in range(1, 5):
        for ch in range(2):
            fwd[ch] = z_shift(fwd[ch], 1)
            bufs[ch][k] = fwd[ch]
            if k < 4:
                bwd[ch] = z_shift(bwd[ch], -1)
                bufs[ch][8 - k] = bwd[ch]
    par = [[None] * 8 for _ in range(2)]
    par[0][0] = par[1][0] = c_swap(jnp.concatenate(first, axis=0))
    for ch in range(2):
        for k in range(1, 8):
            par[ch][k] = c_swap(bufs[ch][k])

    ht, _ = barrier(jnp.swapaxes(hidden, 1, 2), first[1])
    other = y_swap(ht)
    same = yh == ci
    hid = jnp.concatenate([jnp.where(same, ht, other), jnp.where(same, other, ht)], axis=0)
    hg = hgram(hid).reshape(2, 8, TOK, TOK)
    hg = pltpu.with_memory_space_constraint(hg, pltpu.HBM)

    w_own, _ = barrier(w_down, first[1])
    ws = [w_own]
    for k in range(1, 4):
        ws.append(x_shift(w_own, k))
    zc = jnp.stack([zi, ci]).astype(jnp.int32)
    part = jnp.zeros((64, TOK), F32)
    g = [None, None]
    for ch in range(2):
        g[ch], part = gram(ch, zc, bufs[ch], par[ch], hg, part)
    g = [pltpu.with_memory_space_constraint(v, pltpu.HBM) for v in g]
    norms = lax.all_to_all(part, ("yh", "z", "yl", "c"), 0, 0, tiled=True)
    *ws, _ = barrier(*ws, part)
    tails = [w[:, MAIN:] for w in ws]
    nat = []
    for x in range(4):
        v = tails[(0 - x) % 4]
        for me in (1, 2, 3):
            v = jnp.where(xi == me, tails[(me - x) % 4], v)
        nat.append(v)
    wt = jnp.concatenate(nat, axis=1)
    radius = math.sqrt(units * 32 * width / (seqs * 8))

    pieces = {}
    pieces[2], a = wgrad_first(lax.rem(xi + 2, 4), ci, g[0], g[1], hid, norms, radius)
    pieces[1], pieces[3] = wgrad_next([lax.rem(xi + k, 4) for k in (1, 3)], g[0], g[1], a, BF16)
    parts = list(wgrad_next([xi], g[0], g[1], a, F32))
    for k in (2, 1, 3):
        parts.append(x_shift(pieces[k], k))
    weight_grad = total(parts)

    mine = jnp.where(same, 0, 1)
    theirs = dhid(jnp.stack([1 - mine, xi]).astype(jnp.int32), g, ws, wt)
    theirs = y_swap(theirs)
    d_hidden = dhid(jnp.stack([mine, xi]).astype(jnp.int32), g, ws, wt, theirs)
    return weight_grad, jnp.swapaxes(d_hidden, 1, 2)


def solution(mesh):
    fine = Mesh(mesh.devices.reshape(4, 2, 8, 2, 2), ("x", "yh", "z", "yl", "c"))
    dp, mp = ("x", "yh"), ("z", "yl", "c")
    in_specs = (P(dp, None, mp), P(dp, mp, None), P(mp, dp), P(dp))
    out_specs = (P(mp, dp), P(dp, None, mp))

    return jax.shard_map(body, mesh=fine, in_specs=in_specs, out_specs=out_specs, check_vma=False)
```
